128 devices in a mesh: row: 4 (over x), col: 32 (over y, z, core).
Axes of the slice: x: 4, y: 4, z: 4, core: 2. Of those that a mesh axis runs over, the one named last changes fastest.
Arguments:
- ancestor_inverse: float32 [16384, 16384], P('col', 'row'), as said below
- panels: float32 [2, 16384, 512], P(None, ('col', 'row')), may hold values from -0.1875 to 0.1875
- pattern: int32 [2, 128, 2], replicated, may hold values 0 or 1
- diag_inverse: float32 [2, 512, 512], replicated, may hold values from -6 to 6
- link_panel: float32 [512, 512], replicated, may hold values from -0.25 to 0.25
- block_list: int32 [32, 4, 32], P('col', 'row'), may hold values from 0 to 7
- gauge_owner: int32 [32, 4, 32], P('col', 'row'), may hold values from 0 to 31, each once within a row
- gauge_weight: float32 [4, 32, 512], P('row', 'col'), may hold values from -0.25 to 0.25
Outputs:
- y_first: float32 [16384, 512], P(('col', 'row'))
- diag_first: float32 [512, 512], replicated
- y_second: float32 [16384, 512], P(('col', 'row'))
- cross_second: float32 [512, 512], replicated
- diag_second: float32 [512, 512], replicated
- gauge_response: float32 [4, 32, 512], P('row', 'col')
The draws below stay inside these ranges and needn't reach their ends.
Inputs may be any that keep to these rules, and one draw needn't show every extreme that they name: `ancestor_inverse`: with its columns put in natural order the matrix is symmetric.
All inputs are finite; a program needn't handle non-finite values.
Results may differ from the reference program's by a relative error of at most 0.000092.
Values sent between devices are 32-bit elements; how exact they have to be, the bound alone decides.
No kernel may reach another device: no remote copies, remote signals or barrier semaphores. Data moves between devices by JAX's collectives and lax.ppermute only.
A program may use at most 128 MiB of HBM per device.

```python
import math
import jax
import jax.numpy as jnp
from jax import lax

B = 256
KS = 2
SEG = 128
NIB = 8
GRID_R = 4
GRID_C = 32
NSEG = 128
MB = 16384
KB = 512
IBR = 16


def draw_ancestor_inverse(key, part):
    first_key = jax.random.fold_in(key, 0)
    base_values = jax.random.normal(first_key, (MB, MB), jnp.float32)
    natural = (base_values + base_values.T) * (0.70710678 / math.sqrt(MB)) + 3.0 * jnp.eye(MB, dtype=jnp.float32)
    return natural.reshape(MB, GRID_C, GRID_R, SEG).transpose(0, 2, 1, 3).reshape(MB, MB)


def with_ends(values, key, least, largest):
    place = [jax.random.randint(jax.random.fold_in(key, axis), (), 0, length) for axis, length in enumerate(values.shape)]
    widest = values.shape.index(max(values.shape))
    next_to = place[:widest] + [(place[widest] + 1) % values.shape[widest]] + place[widest + 1:]
    return values.at[tuple(place)].set(least).at[tuple(next_to)].set(largest)


def shard_levels(rng, dims, pieces, low, largest):
    def one(axis_at, blocks):
        draws = jax.random.uniform(jax.random.fold_in(jax.random.fold_in(rng, 6), axis_at), (blocks,), jnp.float32, low / len(pieces), largest / len(pieces))
        return jnp.repeat(jnp.exp(draws), dims[axis_at] // blocks).reshape((-1,) + (1,) * (len(dims) - axis_at - 1))

    gain = one(*pieces[0])
    for cut in pieces[1:]:
        gain = gain * one(*cut)
    return gain


def gaussian(stream_key, dims, width, most, pieces=(), held_as=jnp.bfloat16):
    gain = shard_levels(stream_key, dims, pieces, -0.22, 0.18) if pieces else 1.0
    entries = jax.random.normal(stream_key, dims, jnp.float32) * width * gain
    return jnp.minimum(jnp.maximum(entries, -most), most).astype(held_as)


def setup_inputs(seed: int = 0) -> dict:
    splits = jax.random.split(jax.random.key(seed), 9)
    return {
        "ancestor_inverse": draw_ancestor_inverse(jax.random.fold_in(splits[8], 71), 0),
        "panels": gaussian(splits[1], (2, MB, KB), (MB // 16) ** -0.5, 0.1875, ((1, 128),), jnp.float32),
        "pattern": with_ends((jax.random.randint(splits[2], (2, NSEG, KS), 0, 4) < 3).astype(jnp.int32), jax.random.fold_in(splits[2], 1), 0, 1),
        "diag_inverse": gaussian(splits[3], (2, KB, KB), 1.0, 6.0, (), jnp.float32),
        "link_panel": gaussian(splits[4], (KB, KB), KB ** -0.5, 0.25, (), jnp.float32),
        "block_list": with_ends(jax.random.randint(splits[5], (GRID_C, GRID_R, GRID_C), 0, NIB), jax.random.fold_in(splits[5], 1), 0, NIB - 1).astype(jnp.int32),
        "gauge_owner": jax.vmap(lambda own: jax.random.permutation(own, GRID_C))(jax.random.split(splits[6], GRID_C * GRID_R)).reshape((GRID_C, GRID_R, GRID_C)).astype(jnp.int32),
        "gauge_weight": gaussian(splits[7], (GRID_R, GRID_C, GRID_C * IBR), (GRID_C * IBR) ** -0.5, 0.25, ((0, 4), (1, 32)), jnp.float32),
    }


HIGHEST_PRECISION = lax.Precision.HIGHEST


def matmul(left, right):
    return jnp.dot(left, right, precision=HIGHEST_PRECISION, preferred_element_type=jnp.float32)


def reference(ancestor_inverse, panels, pattern, diag_inverse, link_panel, block_list, gauge_owner, gauge_weight):
    natural_inverse = ancestor_inverse.reshape(MB, GRID_R, GRID_C, SEG).transpose(0, 2, 1, 3).reshape(MB, MB)
    tile_flags = pattern.astype(jnp.float32)
    masked_panels = (panels.reshape(2, NSEG, SEG, KS, B) * tile_flags[:, :, None, :, None]).reshape(2, MB, KB)
    first_panel = masked_panels[0]
    second_panel = masked_panels[1]
    y_first = -matmul(natural_inverse, first_panel)
    diag_first = diag_inverse[0] - matmul(first_panel.T, y_first)
    cross_second = -(matmul(y_first.T, second_panel) + matmul(diag_first, link_panel))
    y_second = -(matmul(natural_inverse, second_panel) + matmul(y_first, link_panel))
    diag_second = diag_inverse[1] - matmul(second_panel.T, y_second) - matmul(link_panel.T, cross_second)
    owner_match = (gauge_owner[..., None] == jnp.arange(GRID_C, dtype=jnp.int32)).astype(jnp.float32)
    block_match = (block_list[..., None] == jnp.arange(NIB, dtype=jnp.int32)).astype(jnp.float32)
    selector = jnp.einsum("crke,crkj->crej", owner_match, block_match, precision=HIGHEST_PRECISION)
    segments = y_second.reshape(GRID_C, GRID_R, NIB, IBR * KB)
    chosen = jnp.einsum("crej,crjx->crex", selector, segments, precision=HIGHEST_PRECISION)
    chosen = chosen.reshape(GRID_C, GRID_R, GRID_C, IBR, KB)
    weights = gauge_weight.reshape(GRID_R, GRID_C, GRID_C, IBR)
    gauge_response = jnp.einsum("reci,creit->ret", weights, chosen, precision=HIGHEST_PRECISION)
    return y_first, diag_first, y_second, cross_second, diag_second, gauge_response
```

```python
import jax
import jax.numpy as jnp
from jax import lax
from jax.sharding import Mesh, PartitionSpec as P

NIB = 8
IBR = 16
HIGH = lax.Precision.HIGH
COL = ("y", "z", "core")
CHIPS = ("x", "y", "z")


def dot(left, right, left_dim=1, right_dim=0, precision=HIGH):
    return lax.dot_general(
        left,
        right,
        (((left_dim,), (right_dim,)), ((), ())),
        precision=precision,
        preferred_element_type=jnp.float32,
    )


def swap_core(value):
    return lax.ppermute(value, "core", [(0, 1), (1, 0)])


def spread(value, axes, count):
    copies = jnp.broadcast_to(value[None], (count,) + value.shape)
    return lax.all_to_all(copies, axes, 0, 0, tiled=True)


def all_sum(partial):
    rows, width = partial.shape
    core = lax.axis_index("core")
    halves = partial.reshape(2, rows // 2, width)
    mine = lax.dynamic_index_in_dim(halves, core, 0, keepdims=False)
    theirs = lax.dynamic_index_in_dim(halves, 1 - core, 0, keepdims=False)
    half = mine + swap_core(theirs)
    pieces = half.reshape(64, rows // 128, width)
    part = lax.all_to_all(pieces, CHIPS, 0, 0, tiled=True).sum(0)
    whole = spread(part, CHIPS, 64).reshape(rows // 2, width)
    other = swap_core(whole)
    first = core == 0
    return jnp.concatenate([jnp.where(first, whole, other), jnp.where(first, other, whole)], 0)


def local(
    ancestor,
    panels,
    pattern,
    diag_inverse,
    link,
    block_list,
    gauge_owner,
    gauge_weight,
):
    row = lax.axis_index("x")
    col = lax.axis_index("y") * 8 + lax.axis_index("z") * 2 + lax.axis_index("core")
    flags = lax.dynamic_index_in_dim(pattern, col * 4 + row, 1, keepdims=False)
    flags = jnp.repeat(flags.astype(jnp.float32), 256, axis=1)
    masked = panels * flags[:, None, :]
    both = jnp.concatenate([masked[0], masked[1]], axis=1)
    gathered = lax.all_gather(both, COL, axis=0, tiled=True)
    own_rows = spread(both, "x", 4).reshape(512, 1024)
    weights = lax.all_to_all(gauge_weight.reshape(32, IBR), COL, 0, 0, tiled=True)
    owner_match = (
        gauge_owner[0, 0][None, :] == jnp.arange(32, dtype=jnp.int32)[:, None]
    ).astype(jnp.float32)
    block_match = (
        block_list[0, 0][:, None] == jnp.arange(NIB, dtype=jnp.int32)[None, :]
    ).astype(jnp.float32)
    selector = dot(owner_match, block_match, precision=lax.Precision.HIGHEST)
    combine = (selector[:, :, None] * weights[:, None, :]).reshape(32, NIB * IBR)

    z = dot(ancestor, gathered)
    g_first = dot(own_rows[:, :512], z[:, :512], 0, 0)
    g_cross = dot(z[:, :512], own_rows[:, 512:], 0, 0)
    g_second = dot(own_rows[:, 512:], z[:, 512:], 0, 0)
    z_rows = lax.all_to_all(z.reshape(4, 128, 1024), "x", 0, 0, tiled=True).sum(0)
    grams = all_sum(jnp.concatenate([g_first, g_cross, g_second], 0))
    y_first = -z_rows[:, :512]
    y_second = -(z_rows[:, 512:] + dot(y_first, link))
    shares = dot(combine, y_second)
    gauge = lax.all_to_all(shares, COL, 0, 0, tiled=True).sum(0).reshape(1, 1, 512)
    diag_first = diag_inverse[0] + grams[:512]
    cross = grams[512:1024]
    cross_second = cross - dot(diag_first, link)
    diag_second = (
        diag_inverse[1] + grams[1024:] - dot(cross, link, 0, 0) - dot(link, cross_second, 0, 0)
    )
    return (y_first, diag_first, y_second, cross_second, diag_second, gauge)


def solution(mesh):
    grid = Mesh(mesh.devices.reshape(4, 4, 4, 2), ("x", "y", "z", "core"))
    in_specs = (
        P(COL, "x"),
        P(None, COL + ("x",), None),
        P(),
        P(),
        P(),
        P(COL, "x", None),
        P(COL, "x", None),
        P("x", COL, None),
    )
    out_specs = (
        P(COL + ("x",), None),
        P(),
        P(COL + ("x",), None),
        P(),
        P(),
        P("x", COL, None),
    )
    return jax.shard_map(local, mesh=grid, in_specs=in_specs, out_specs=out_specs, check_vma=False)
```

```python
import functools

import jax
import jax.numpy as jnp
from jax import lax
from jax.experimental import pallas as pl
from jax.experimental.pallas import tpu as pltpu
from jax.sharding import Mesh, PartitionSpec as P

NIB = 8
IBR = 16
HIGH = lax.Precision.HIGH
HIGHEST = lax.Precision.HIGHEST
COL = ("y", "z", "core")
CHIPS = ("x", "y", "z")
F32 = jnp.float32
BF16 = jnp.bfloat16


def dot(left, right, left_dim=1, right_dim=0, precision=HIGH):
    return lax.dot_general(
        left,
        right,
        (((left_dim,), (right_dim,)), ((), ())),
        precision=precision,
        preferred_element_type=F32,
    )


def swap_core(value):
    return lax.ppermute(value, "core", [(0, 1), (1, 0)])


def hop(value, leg, step):
    pairs = []
    for y in range(4):
        for z in range(4):
            for core in range(2):
                along_z = core == leg
                to_y, to_z = (y, (z + step) % 4) if along_z else ((y + step) % 4, z)
                pairs.append((y * 8 + z * 2 + core, to_y * 8 + to_z * 2 + core))
    return lax.ppermute(value, COL, pairs)


def parts(value):
    high = value.astype(BF16)
    return high, (value - high.astype(F32)).astype(BF16)


def product_kernel(count, has_total, order, mine, other, *refs):
    pieces = refs[:count]
    out, piece_high, piece_low = refs[-3:]
    step = pl.program_id(0)
    core = order[pl.num_programs(0)]

    @pl.when(step == 0)
    def _():
        at = 0
        for piece in pieces:
            rows = piece.shape[0]
            piece_high[at : at + rows, :], piece_low[at : at + rows, :] = parts(piece[...])
            at += rows
        out[...] = refs[count][...] if has_total else jnp.zeros_like(out)

    at = pl.ds(pl.multiple_of(step * 256, 256), 256)
    high, low = piece_high[at, :], piece_low[at, :]
    right = jnp.concatenate([high, low, high], axis=0)
    for source, side in ((mine, core), (other, 1 - core)):
        top, rest = parts(source[...])
        left = jnp.concatenate([top, top, rest], axis=1)
        made = jnp.dot(left, right, preferred_element_type=F32)
        for row in range(4):
            to = pl.ds(pl.multiple_of(row * 256 + side * 128, 128), 128)
            out[to, :] += made[row * 128 : row * 128 + 128, :]


def add_product(order, mine, other, pieces, total=None):
    depth = sum(piece.shape[0] for piece in pieces)
    block = pl.BlockSpec((512, 256), lambda j, order: (0, order[j]))
    whole = [pl.BlockSpec(piece.shape, lambda j, order: (0, 0)) for piece in pieces]
    made = pl.BlockSpec((1024, 512), lambda j, order: (0, 0))
    has_total = total is not None
    args = [order, mine, other, *pieces] + ([total] if has_total else [])
    return pl.pallas_call(
        functools.partial(product_kernel, len(pieces), has_total),
        grid_spec=pltpu.PrefetchScalarGridSpec(
            num_scalar_prefetch=1,
            grid=(depth // 256,),
            in_specs=[block, block, *whole] + ([made] if has_total else []),
            out_specs=made,
            scratch_shapes=[pltpu.VMEM((depth, 512), BF16)] * 2,
        ),
        out_shape=jax.ShapeDtypeStruct((1024, 512), F32),
        cost_estimate=pl.CostEstimate(
            flops=6 * 1024 * 512 * depth, bytes_accessed=5120 * depth, transcendentals=0
        ),
    )(*args)


def gram_kernel(rows, z, out):
    rows_high, rows_low = parts(rows[...])
    z_high, z_low = parts(z[...])

    def product(left, right):
        return lax.dot_general(left, right, (((0,), (0,)), ((), ())), preferred_element_type=F32)

    def gram(at, to):
        return (
            product(rows_high[:, at], z_high[:, to])
            + product(rows_high[:, at], z_low[:, to])
            + product(rows_low[:, at], z_high[:, to])
        )

    @pl.when(pl.program_id(0) == 0)
    def _():
        out[...] = jnp.zeros_like(out)

    out[:, :512] += gram(slice(0, 512), slice(0, 512))
    out[:, 512:] += gram(slice(512, 1024), slice(256, 512))


def grams_of(rows, z):
    return pl.pallas_call(
        gram_kernel,
        grid=(4,),
        in_specs=[
            pl.BlockSpec((256, 1024), lambda k: (k, 0)),
            pl.BlockSpec((256, 512), lambda k: (k, 0)),
        ],
        out_specs=pl.BlockSpec((512, 768), lambda k: (0, 0)),
        out_shape=jax.ShapeDtypeStruct((512, 768), F32),
        cost_estimate=pl.CostEstimate(
            flops=6 * 1024 * 512 * 768, bytes_accessed=7 << 20, transcendentals=0
        ),
    )(rows, z)


def local(
    ancestor,
    panels,
    pattern,
    diag_inverse,
    link,
    block_list,
    gauge_owner,
    gauge_weight,
):
    row = lax.axis_index("x")
    place_y, place_z, core = (lax.axis_index(name) for name in COL)
    first = core == 0
    col = place_y * 8 + place_z * 2 + core
    flags = lax.dynamic_index_in_dim(pattern, col * 4 + row, 1, keepdims=False).astype(F32)
    tiles = panels.reshape(2, 128, 2, 256) * flags[:, None, :, None]
    left, right = tiles[:, :, 0], tiles[:, :, 1]
    theirs = swap_core(jnp.where(first, right, left))
    mine = jnp.where(first, left, right)
    own = jnp.concatenate([jnp.where(first, mine, theirs), jnp.where(first, theirs, mine)], axis=1)
    ancestor, theirs = lax.optimization_barrier((ancestor, theirs))
    other = swap_core(ancestor)

    def order_of(*offsets):
        order = []
        for leg_0, leg_1 in offsets:
            step_y = jnp.where(first, leg_1, leg_0)
            step_z = jnp.where(first, leg_0, leg_1)
            order.append(((place_y + step_y) % 4) * 4 + (place_z + step_z) % 4)
        return jnp.stack(order + [core]).astype(jnp.int32)

    both = jnp.concatenate([left[0], right[0], left[1], right[1]], axis=1)
    rows = lax.all_gather(both, ("x", "core"), axis=0, tiled=True)
    weights = jnp.broadcast_to(gauge_weight.reshape(1, 512), (8, 512))
    weights, rows = lax.optimization_barrier((weights, rows))
    weights = lax.all_gather(weights, COL, axis=0, tiled=True).reshape(32, 8, 512)[:, 0]
    weights = lax.dynamic_slice_in_dim(weights, col * IBR, IBR, axis=1)
    owner_match = (
        gauge_owner[0, 0][None, :] == jnp.arange(32, dtype=jnp.int32)[:, None]
    ).astype(F32)
    block_match = (
        block_list[0, 0][:, None] == jnp.arange(NIB, dtype=jnp.int32)[None, :]
    ).astype(F32)
    selector = dot(owner_match, block_match, precision=HIGHEST)
    combine = (selector[:, :, None] * weights[:, None, :]).reshape(32, NIB * IBR)
    own = jnp.concatenate([own[0], own[1]], axis=1)
    behind = hop(own, 0, 1)
    ahead = hop(own, 0, -1)
    across = hop(own, 0, 2)
    pair = jnp.concatenate([own, behind], axis=0)
    pair_behind = hop(pair, 1, 1)
    pair_ahead = hop(pair, 1, -1)
    rest = jnp.concatenate([ahead, across], axis=0)
    rest_behind = hop(rest, 1, 1)
    rest_ahead = hop(rest, 1, -1)
    z = add_product(order_of((0, 0), (-1, 0), (1, 0), (2, 0)), ancestor, other, (pair, rest))
    pair_behind, z = lax.optimization_barrier((pair_behind, z))
    pair_across = hop(pair_behind, 1, 1)
    z = add_product(
        order_of((0, -1), (-1, -1), (0, 1), (-1, 1)), ancestor, other, (pair_behind, pair_ahead), z
    )
    rest_ahead, z = lax.optimization_barrier((rest_ahead, z))
    rest_across = hop(rest_ahead, 1, -1)
    z = add_product(
        order_of((1, -1), (2, -1), (1, 1), (2, 1), (0, 2), (-1, 2)),
        ancestor,
        other,
        (rest_behind, rest_ahead, pair_across),
        z,
    )
    z, rows = lax.optimization_barrier((z, rows))
    z = add_product(order_of((1, 2), (2, 2)), ancestor, other, (rest_across,), z)

    z_pair = lax.psum_scatter(z, "x", scatter_dimension=0, tiled=True)
    grams = grams_of(rows, z)
    part = lax.all_to_all(grams.reshape(64, 8, 768), CHIPS, 0, 0, tiled=True).sum(0)

    z_mine = jnp.where(first, z_pair[:128], z_pair[128:])
    z_theirs = swap_core(jnp.where(first, z_pair[128:], z_pair[:128]))
    z_left = jnp.where(first, z_mine, z_theirs)
    z_right = jnp.where(first, z_theirs, z_mine)
    y_first = -jnp.concatenate([z_left[:, :256], z_right[:, :256]], axis=1)
    z_second = jnp.concatenate([z_left[:, 256:], z_right[:, 256:]], axis=1)
    y_second = -(z_second + dot(y_first, link))
    shares = dot(combine, y_second).reshape(1, 16, 8, 128)
    here = lax.broadcasted_iota(jnp.int32, (4, 1, 1, 1), 0) == row
    shares = jnp.where(here, shares, 0.0).reshape(64, 8, 128)
    message = jnp.concatenate([jnp.broadcast_to(part[None], (64, 8, 768)), shares], axis=2)
    message = lax.all_to_all(message, CHIPS, 0, 0, tiled=True)
    gauge = message[:, :, 768:].sum(0).reshape(2, 512)
    gauge = jnp.where(first, gauge[:1], gauge[1:]) + swap_core(
        jnp.where(first, gauge[1:], gauge[:1])
    )
    whole = message[:, :, :768].reshape(512, 768)
    others = swap_core(whole)
    left = jnp.where(first, whole, others)
    right = jnp.where(first, others, whole)

    def gram(slot):
        at = slice(slot * 256, slot * 256 + 256)
        return jnp.concatenate([left[:, at], right[:, at]], axis=1)

    diag_first = diag_inverse[0] + gram(0)
    cross = gram(1)
    cross_second = cross - dot(diag_first, link)
    diag_second = (
        diag_inverse[1] + gram(2) - dot(cross, link, 0, 0) - dot(link, cross_second, 0, 0)
    )
    return (y_first, diag_first, y_second, cross_second, diag_second, gauge.reshape(1, 1, 512))


def solution(mesh):
    grid = Mesh(mesh.devices.reshape(4, 4, 4, 2), CHIPS + ("core",))
    in_specs = (
        P(COL, "x"),
        P(None, COL + ("x",), None),
        P(),
        P(),
        P(),
        P(COL, "x", None),
        P(COL, "x", None),
        P("x", COL, None),
    )
    out_specs = (
        P(COL + ("x",), None),
        P(),
        P(COL + ("x",), None),
        P(),
        P(),
        P("x", COL, None),
    )
    return jax.shard_map(local, mesh=grid, in_specs=in_specs, out_specs=out_specs, check_vma=False)
```

```python
import functools

import jax
import jax.numpy as jnp
from jax import lax
from jax.experimental import pallas as pl
from jax.experimental.pallas import tpu as pltpu
from jax.sharding import Mesh, PartitionSpec as P

NIB = 8
IBR = 16
HIGH = lax.Precision.HIGH
HIGHEST = lax.Precision.HIGHEST
COL = ("y", "z", "core")
CHIPS = ("x", "y", "z")
F32 = jnp.float32
BF16 = jnp.bfloat16


def dot(left, right, left_dim=1, right_dim=0, precision=HIGH):
    return lax.dot_general(
        left,
        right,
        (((left_dim,), (right_dim,)), ((), ())),
        precision=precision,
        preferred_element_type=F32,
    )


def swap_core(value):
    return lax.ppermute(value, "core", [(0, 1), (1, 0)])


def hop(value, leg, step):
    pairs = []
    for y in range(4):
        for z in range(4):
            for core in range(2):
                along_z = core == leg
                to_y, to_z = (y, (z + step) % 4) if along_z else ((y + step) % 4, z)
                pairs.append((y * 8 + z * 2 + core, to_y * 8 + to_z * 2 + core))
    return lax.ppermute(value, COL, pairs)


def parts(value):
    high = value.astype(BF16)
    return high, (value - high.astype(F32)).astype(BF16)


def product_kernel(count, has_total, order, mine, other, *refs):
    pieces = refs[:count]
    out, piece_high, piece_low = refs[-3:]
    step = pl.program_id(0)
    core = order[pl.num_programs(0)]

    @pl.when(step == 0)
    def _():
        at = 0
        for piece in pieces:
            rows = piece.shape[0]
            piece_high[at : at + rows, :], piece_low[at : at + rows, :] = parts(piece[...])
            at += rows
        out[...] = refs[count][...] if has_total else jnp.zeros_like(out)

    at = pl.ds(pl.multiple_of(step * 256, 256), 256)
    high, low = piece_high[at, :], piece_low[at, :]
    right = jnp.concatenate([high, low, high], axis=0)
    for source, side in ((mine, core), (other, 1 - core)):
        top, rest = parts(source[...])
        left = jnp.concatenate([top, top, rest], axis=1)
        made = jnp.dot(left, right, preferred_element_type=F32)
        for row in range(4):
            to = pl.ds(pl.multiple_of(row * 256 + side * 128, 128), 128)
            out[to, :] += made[row * 128 : row * 128 + 128, :]


def add_product(order, mine, other, pieces, total=None):
    depth = sum(piece.shape[0] for piece in pieces)
    block = pl.BlockSpec((512, 256), lambda j, order: (0, order[j]))
    whole = [pl.BlockSpec(piece.shape, lambda j, order: (0, 0)) for piece in pieces]
    made = pl.BlockSpec((1024, 512), lambda j, order: (0, 0))
    has_total = total is not None
    args = [order, mine, other, *pieces] + ([total] if has_total else [])
    return pl.pallas_call(
        functools.partial(product_kernel, len(pieces), has_total),
        grid_spec=pltpu.PrefetchScalarGridSpec(
            num_scalar_prefetch=1,
            grid=(depth // 256,),
            in_specs=[block, block, *whole] + ([made] if has_total else []),
            out_specs=made,
            scratch_shapes=[pltpu.VMEM((depth, 512), BF16)] * 2,
        ),
        out_shape=jax.ShapeDtypeStruct((1024, 512), F32),
        cost_estimate=pl.CostEstimate(
            flops=6 * 1024 * 512 * depth, bytes_accessed=5120 * depth, transcendentals=0
        ),
    )(*args)


def gram_kernel(core, rows, z, out):
    rows_high, rows_low = parts(rows[...])
    z_high, z_low = parts(z[...])
    first = core[0] == 0

    def product(left, right):
        def terms(one, two):
            return lax.dot_general(one, two, (((0,), (0,)), ((), ())), preferred_element_type=F32)

        return terms(left[0], right[0]) + terms(left[0], right[1]) + terms(left[1], right[0])

    def panel(start, stop):
        return rows_high[:, start:stop], rows_low[:, start:stop]

    def kept(start, stop):
        return z_high[:, start:stop], z_low[:, start:stop]

    def either(one, two):
        return tuple(jnp.where(first, left, right) for left, right in zip(one, two))

    @pl.when(pl.program_id(0) == 0)
    def _():
        out[...] = jnp.zeros_like(out)

    out[:, :256] += product(panel(0, 512), kept(256, 512))
    for slot in range(2):
        at, start, half = slice(slot * 256, slot * 256 + 256), slot * 512, slot * 256
        low, high = panel(start, start + 256), panel(start + 256, start + 512)
        mine = kept(half, half + 256)
        out[at, 256:512] += product(either(low, high), mine)
        out[at, 512:] += product(
            either(high, mine), either(kept(half, half + 128), panel(start + 128, start + 256))
        )


def grams_of(core, rows, z):
    return pl.pallas_call(
        gram_kernel,
        grid_spec=pltpu.PrefetchScalarGridSpec(
            num_scalar_prefetch=1,
            grid=(4,),
            in_specs=[
                pl.BlockSpec((256, 1024), lambda k, core: (k, 0)),
                pl.BlockSpec((256, 512), lambda k, core: (k, 0)),
            ],
            out_specs=pl.BlockSpec((512, 640), lambda k, core: (0, 0)),
        ),
        out_shape=jax.ShapeDtypeStruct((512, 640), F32),
        cost_estimate=pl.CostEstimate(
            flops=6 * 1024 * 512 * 640, bytes_accessed=7 << 20, transcendentals=0
        ),
    )(core, rows, z)


def close_kernel(core, mine, theirs, diag, link, diag_first, cross_second, diag_second):
    first = core[0] == 0

    def sides(rows, columns):
        kept, came = mine[rows, columns], theirs[rows, columns]
        return jnp.where(first, kept, came), jnp.where(first, came, kept)

    def symmetric(slot):
        rows = slice(slot * 256, slot * 256 + 256)
        upper, lower = sides(rows, slice(256, 512))
        below = jnp.concatenate(sides(rows, slice(512, 640)), axis=1)
        return jnp.concatenate(
            [
                jnp.concatenate([upper, below.T], axis=1),
                jnp.concatenate([below, lower], axis=1),
            ],
            axis=0,
        )

    def product(left, right, dim=1):
        def terms(one, two):
            return lax.dot_general(one, two, (((dim,), (0,)), ((), ())), preferred_element_type=F32)

        left, right = parts(left), parts(right)
        return terms(left[0], right[0]) + terms(left[0], right[1]) + terms(left[1], right[0])

    cross = jnp.concatenate(sides(slice(0, 512), slice(0, 256)), axis=1)
    links = link[...]
    top = diag[0] + symmetric(0)
    diag_first[...] = top
    second = cross - product(top, links)
    cross_second[...] = second
    diag_second[...] = (
        diag[1] + symmetric(1) - product(cross, links, 0) - product(links, second, 0)
    )


def close(core, mine, theirs, diag, link):
    return pl.pallas_call(
        close_kernel,
        in_specs=[pl.BlockSpec(memory_space=pltpu.SMEM)]
        + [pl.BlockSpec(memory_space=pltpu.VMEM)] * 4,
        out_shape=[jax.ShapeDtypeStruct((512, 512), F32)] * 3,
        cost_estimate=pl.CostEstimate(
            flops=36 * 512 * 512 * 512, bytes_accessed=9 << 20, transcendentals=0
        ),
    )(core, mine, theirs, diag, link)


def local(
    ancestor,
    panels,
    pattern,
    diag_inverse,
    link,
    block_list,
    gauge_owner,
    gauge_weight,
):
    row = lax.axis_index("x")
    place_y, place_z, core = (lax.axis_index(name) for name in COL)
    first = core == 0
    col = place_y * 8 + place_z * 2 + core
    flags = lax.dynamic_index_in_dim(pattern, col * 4 + row, 1, keepdims=False).astype(F32)
    tiles = panels.reshape(2, 128, 2, 256) * flags[:, None, :, None]
    left, right = tiles[:, :, 0], tiles[:, :, 1]
    theirs = swap_core(jnp.where(first, right, left))
    mine = jnp.where(first, left, right)
    own = jnp.concatenate([jnp.where(first, mine, theirs), jnp.where(first, theirs, mine)], axis=1)
    ancestor, theirs = lax.optimization_barrier((ancestor, theirs))
    other = swap_core(ancestor)

    def order_of(*offsets):
        order = []
        for leg_0, leg_1 in offsets:
            step_y = jnp.where(first, leg_1, leg_0)
            step_z = jnp.where(first, leg_0, leg_1)
            order.append(((place_y + step_y) % 4) * 4 + (place_z + step_z) % 4)
        return jnp.stack(order + [core]).astype(jnp.int32)

    both = jnp.concatenate([left[0], right[0], left[1], right[1]], axis=1)
    rows = lax.all_gather(both, ("x", "core"), axis=0, tiled=True)
    own = jnp.concatenate([own[0], own[1]], axis=1)
    behind = hop(own, 0, 1)
    ahead = hop(own, 0, -1)
    across = hop(own, 0, 2)
    weights = jnp.broadcast_to(gauge_weight.reshape(1, 512), (16, 512))
    weights, behind = lax.optimization_barrier((weights, behind))
    weights = lax.all_gather(weights, COL, axis=0, tiled=True).reshape(32, 16, 512)[:, 0]
    weights = lax.dynamic_slice_in_dim(weights, col * IBR, IBR, axis=1)
    pair = jnp.concatenate([own, behind], axis=0)
    pair_behind = hop(pair, 1, 1)
    pair_ahead = hop(pair, 1, -1)
    rest = jnp.concatenate([ahead, across], axis=0)
    rest_behind = hop(rest, 1, 1)
    rest_ahead = hop(rest, 1, -1)
    z = add_product(order_of((0, 0), (-1, 0), (1, 0), (2, 0)), ancestor, other, (pair, rest))
    pair_behind, z = lax.optimization_barrier((pair_behind, z))
    pair_across = hop(pair_behind, 1, 1)
    z = add_product(
        order_of((0, -1), (-1, -1), (0, 1), (-1, 1)), ancestor, other, (pair_behind, pair_ahead), z
    )
    rest_ahead, z = lax.optimization_barrier((rest_ahead, z))
    rest_across = hop(rest_ahead, 1, -1)
    z = add_product(
        order_of((1, -1), (2, -1), (1, 1), (2, 1), (0, 2), (-1, 2)),
        ancestor,
        other,
        (rest_behind, rest_ahead, pair_across),
        z,
    )
    z, rows = lax.optimization_barrier((z, rows))
    z = add_product(order_of((1, 2), (2, 2)), ancestor, other, (rest_across,), z)

    owner_match = (
        gauge_owner[0, 0][None, :] == jnp.arange(32, dtype=jnp.int32)[:, None]
    ).astype(F32)
    block_match = (
        block_list[0, 0][:, None] == jnp.arange(NIB, dtype=jnp.int32)[None, :]
    ).astype(F32)
    selector = dot(owner_match, block_match, precision=HIGHEST)
    combine = (selector[:, :, None] * weights[:, None, :]).reshape(32, NIB * IBR)
    core_list = core.astype(jnp.int32).reshape(1)
    plane = ("y", "z")
    z_pair = lax.psum_scatter(z, "x", scatter_dimension=0, tiled=True)
    part = grams_of(core_list, rows, z).reshape(16, 32, 640)
    part = lax.all_to_all(part, plane, 0, 0, tiled=True).sum(0)
    part = jnp.broadcast_to(part[None], (4, 32, 640))
    part = lax.all_to_all(part, "x", 0, 0, tiled=True).sum(0)

    z_mine = jnp.where(first, z_pair[:128], z_pair[128:])
    z_theirs = swap_core(jnp.where(first, z_pair[128:], z_pair[:128]))
    z_left = jnp.where(first, z_mine, z_theirs)
    z_right = jnp.where(first, z_theirs, z_mine)
    y_first = -jnp.concatenate([z_left[:, :256], z_right[:, :256]], axis=1)
    z_second = jnp.concatenate([z_left[:, 256:], z_right[:, 256:]], axis=1)
    y_second = -(z_second + dot(y_first, link))
    shares = jnp.pad(dot(combine, y_second).reshape(16, 8, 128), ((0, 0), (0, 24), (0, 0)))
    message = jnp.concatenate([jnp.broadcast_to(part[None], (16, 32, 640)), shares], axis=2)
    message = lax.all_to_all(message, plane, 0, 0, tiled=True)
    gauge = message[:, :8, 640:].sum(0).reshape(2, 512)
    gauge = jnp.where(first, gauge[:1], gauge[1:]) + swap_core(
        jnp.where(first, gauge[1:], gauge[:1])
    )
    whole = message[:, :, :640].reshape(512, 640)
    diag_first, cross_second, diag_second = close(
        core_list, whole, swap_core(whole), diag_inverse, link
    )
    return (y_first, diag_first, y_second, cross_second, diag_second, gauge.reshape(1, 1, 512))


def solution(mesh):
    grid = Mesh(mesh.devices.reshape(4, 4, 4, 2), CHIPS + ("core",))
    in_specs = (
        P(COL, "x"),
        P(None, COL + ("x",), None),
        P(),
        P(),
        P(),
        P(COL, "x", None),
        P(COL, "x", None),
        P("x", COL, None),
    )
    out_specs = (
        P(COL + ("x",), None),
        P(),
        P(COL + ("x",), None),
        P(),
        P(),
        P("x", COL, None),
    )
    return jax.shard_map(local, mesh=grid, in_specs=in_specs, out_specs=out_specs, check_vma=False)
```

```python
import functools

import jax
import jax.numpy as jnp
from jax import lax
from jax.experimental import pallas as pl
from jax.experimental.pallas import tpu as pltpu
from jax.sharding import Mesh, PartitionSpec as P

NIB = 8
IBR = 16
HIGH = lax.Precision.HIGH
HIGHEST = lax.Precision.HIGHEST
COL = ("y", "z", "core")
CHIPS = ("x", "y", "z")
F32 = jnp.float32
BF16 = jnp.bfloat16


def dot(left, right, left_dim=1, right_dim=0, precision=HIGH):
    return lax.dot_general(
        left,
        right,
        (((left_dim,), (right_dim,)), ((), ())),
        precision=precision,
        preferred_element_type=F32,
    )


def swap_core(value):
    return lax.ppermute(value, "core", [(0, 1), (1, 0)])


def hop(value, leg, step):
    pairs = []
    for y in range(4):
        for z in range(4):
            for core in range(2):
                along_z = core == leg
                to_y, to_z = (y, (z + step) % 4) if along_z else ((y + step) % 4, z)
                pairs.append((y * 8 + z * 2 + core, to_y * 8 + to_z * 2 + core))
    return lax.ppermute(value, COL, pairs)


def parts(value):
    high = value.astype(BF16)
    return high, (value - high.astype(F32)).astype(BF16)


def product_kernel(count, has_total, has_gram, order, *refs):
    blocks, refs = refs[:4], refs[4:]
    pieces, refs = refs[:count], refs[count:]
    total, refs = (refs[0], refs[1:]) if has_total else (None, refs)
    rows, refs = (refs[0], refs[1:]) if has_gram else (None, refs)
    out, piece_high, piece_low = refs[0], refs[-2], refs[-1]
    step = pl.program_id(0)
    core = order[2 * pl.num_programs(0)]

    @pl.when(step == 0)
    def _():
        at = 0
        for piece in pieces:
            count_rows = piece.shape[0]
            to = slice(at, at + count_rows)
            piece_high[to, :], piece_low[to, :] = parts(piece[...])
            at += count_rows
        out[...] = total[...] if has_total else jnp.zeros_like(out)

    at = pl.ds(pl.multiple_of(step * 512, 512), 512)
    high, low = piece_high[at, :], piece_low[at, :]
    right = jnp.concatenate([high, low, high], axis=0)
    for one, two, side in ((blocks[0], blocks[1], core), (blocks[2], blocks[3], 1 - core)):
        one, two = parts(one[...]), parts(two[...])
        left = jnp.concatenate([one[0], two[0], one[0], two[0], one[1], two[1]], axis=1)
        made = jnp.dot(left, right, preferred_element_type=F32)
        for row in range(4):
            to = pl.ds(pl.multiple_of(row * 256 + side * 128, 128), 128)
            out[to, :] += made[row * 128 : row * 128 + 128, :]

    if has_gram:

        @pl.when(step == pl.num_programs(0) - 1)
        def _():
            gram_of(core == 0, rows, out, refs[1])


def add_product(order, mine, other, pieces, total=None, rows=None):
    depth = sum(piece.shape[0] for piece in pieces)
    one = pl.BlockSpec((512, 256), lambda j, order: (0, order[2 * j]))
    two = pl.BlockSpec((512, 256), lambda j, order: (0, order[2 * j + 1]))

    def fixed(shape):
        return pl.BlockSpec(shape, lambda j, order: (0, 0))

    made = fixed((1024, 512))
    has_total, has_gram = total is not None, rows is not None
    args = [order, mine, mine, other, other, *pieces]
    in_specs = [one, two, one, two] + [fixed(piece.shape) for piece in pieces]
    out_specs, out_shape = [made], [jax.ShapeDtypeStruct((1024, 512), F32)]
    if has_total:
        args.append(total)
        in_specs.append(made)
    if has_gram:
        args.append(rows)
        in_specs.append(fixed((1024, 1024)))
        out_specs.append(fixed((512, 640)))
        out_shape.append(jax.ShapeDtypeStruct((512, 640), F32))
    made = pl.pallas_call(
        functools.partial(product_kernel, len(pieces), has_total, has_gram),
        grid_spec=pltpu.PrefetchScalarGridSpec(
            num_scalar_prefetch=1,
            grid=(depth // 512,),
            in_specs=in_specs,
            out_specs=out_specs,
            scratch_shapes=[pltpu.VMEM((depth, 512), BF16)] * 2,
        ),
        out_shape=out_shape,
        cost_estimate=pl.CostEstimate(
            flops=6 * 1024 * 512 * depth, bytes_accessed=5120 * depth, transcendentals=0
        ),
        compiler_params=pltpu.CompilerParams(vmem_limit_bytes=48 << 20),
    )(*args)
    return made if has_gram else made[0]


def gram_of(first, rows, z, out):
    rows_high, rows_low = parts(rows[...])
    z_high, z_low = parts(z[...])

    def product(left, right):
        def terms(one, two):
            return lax.dot_general(one, two, (((0,), (0,)), ((), ())), preferred_element_type=F32)

        return terms(left[0], right[0]) + terms(left[0], right[1]) + terms(left[1], right[0])

    def panel(start, stop):
        return rows_high[:, start:stop], rows_low[:, start:stop]

    def kept(start, stop):
        return z_high[:, start:stop], z_low[:, start:stop]

    def either(one, two):
        return tuple(jnp.where(first, left, right) for left, right in zip(one, two))

    out[:, :256] = product(panel(0, 512), kept(256, 512))
    for slot in range(2):
        at, start, half = slice(slot * 256, slot * 256 + 256), slot * 512, slot * 256
        low, high = panel(start, start + 256), panel(start + 256, start + 512)
        mine = kept(half, half + 256)
        out[at, 256:512] = product(either(low, high), mine)
        out[at, 512:] = product(
            either(high, mine), either(kept(half, half + 128), panel(start + 128, start + 256))
        )


def close_kernel(core, mine, theirs, diag, link, diag_first, cross_second, diag_second):
    first = core[0] == 0

    def sides(rows, columns):
        kept, came = mine[rows, columns], theirs[rows, columns]
        return jnp.where(first, kept, came), jnp.where(first, came, kept)

    def symmetric(slot):
        rows = slice(slot * 256, slot * 256 + 256)
        upper, lower = sides(rows, slice(256, 512))
        below = jnp.concatenate(sides(rows, slice(512, 640)), axis=1)
        return jnp.concatenate(
            [
                jnp.concatenate([upper, below.T], axis=1),
                jnp.concatenate([below, lower], axis=1),
            ],
            axis=0,
        )

    def product(left, right, dim=1):
        def terms(one, two):
            return lax.dot_general(one, two, (((dim,), (0,)), ((), ())), preferred_element_type=F32)

        left, right = parts(left), parts(right)
        return terms(left[0], right[0]) + terms(left[0], right[1]) + terms(left[1], right[0])

    cross = jnp.concatenate(sides(slice(0, 512), slice(0, 256)), axis=1)
    links = link[...]
    top = diag[0] + symmetric(0)
    diag_first[...] = top
    second = cross - product(top, links)
    cross_second[...] = second
    diag_second[...] = (
        diag[1] + symmetric(1) - product(cross, links, 0) - product(links, second, 0)
    )


def close(core, mine, theirs, diag, link):
    return pl.pallas_call(
        close_kernel,
        in_specs=[pl.BlockSpec(memory_space=pltpu.SMEM)]
        + [pl.BlockSpec(memory_space=pltpu.VMEM)] * 4,
        out_shape=[jax.ShapeDtypeStruct((512, 512), F32)] * 3,
        cost_estimate=pl.CostEstimate(
            flops=36 * 512 * 512 * 512, bytes_accessed=9 << 20, transcendentals=0
        ),
    )(core, mine, theirs, diag, link)


def local(
    ancestor,
    panels,
    pattern,
    diag_inverse,
    link,
    block_list,
    gauge_owner,
    gauge_weight,
):
    row = lax.axis_index("x")
    place_y, place_z, core = (lax.axis_index(name) for name in COL)
    first = core == 0
    col = place_y * 8 + place_z * 2 + core
    flags = lax.dynamic_index_in_dim(pattern, col * 4 + row, 1, keepdims=False).astype(F32)
    tiles = panels.reshape(2, 128, 2, 256) * flags[:, None, :, None]
    left, right = tiles[:, :, 0], tiles[:, :, 1]
    theirs = swap_core(jnp.where(first, right, left))
    mine = jnp.where(first, left, right)
    own = jnp.concatenate([jnp.where(first, mine, theirs), jnp.where(first, theirs, mine)], axis=1)
    ancestor, theirs = lax.optimization_barrier((ancestor, theirs))
    other = swap_core(ancestor)

    def order_of(*offsets):
        order = []
        for leg_0, leg_1 in offsets:
            step_y = jnp.where(first, leg_1, leg_0)
            step_z = jnp.where(first, leg_0, leg_1)
            order.append(((place_y + step_y) % 4) * 4 + (place_z + step_z) % 4)
        return jnp.stack(order + [core]).astype(jnp.int32)

    both = jnp.concatenate([left[0], right[0], left[1], right[1]], axis=1)
    rows = lax.all_gather(both, ("x", "core"), axis=0, tiled=True)
    own = jnp.concatenate([own[0], own[1]], axis=1)
    behind = hop(own, 0, 1)
    ahead = hop(own, 0, -1)
    across = hop(own, 0, 2)
    pair = jnp.concatenate([own, behind], axis=0)
    pair_behind = hop(pair, 1, 1)
    pair_ahead = hop(pair, 1, -1)
    rest = jnp.concatenate([ahead, across], axis=0)
    rest_behind = hop(rest, 1, 1)
    rest_ahead = hop(rest, 1, -1)
    z = add_product(order_of((0, 0), (-1, 0), (1, 0), (2, 0)), ancestor, other, (pair, rest))
    pair_behind, z = lax.optimization_barrier((pair_behind, z))
    pair_across = hop(pair_behind, 1, 1)
    z = add_product(
        order_of((0, -1), (-1, -1), (0, 1), (-1, 1)), ancestor, other, (pair_behind, pair_ahead), z
    )
    weights = gauge_weight.reshape(32, IBR)
    rest_ahead, z, weights = lax.optimization_barrier((rest_ahead, z, weights))
    rest_across = hop(rest_ahead, 1, -1)
    weights = lax.all_to_all(weights, COL, 0, 0, tiled=True)
    z = add_product(
        order_of((1, -1), (2, -1), (1, 1), (2, 1), (0, 2), (-1, 2)),
        ancestor,
        other,
        (rest_behind, rest_ahead, pair_across),
        z,
    )
    z, rows, weights = lax.optimization_barrier((z, rows, weights))
    z, part = add_product(
        order_of((1, 2), (2, 2)), ancestor, other, (rest_across,), z, rows
    )

    owner_match = (
        gauge_owner[0, 0][None, :] == jnp.arange(32, dtype=jnp.int32)[:, None]
    ).astype(F32)
    block_match = (
        block_list[0, 0][:, None] == jnp.arange(NIB, dtype=jnp.int32)[None, :]
    ).astype(F32)
    selector = dot(owner_match, block_match, precision=HIGHEST)
    combine = (selector[:, :, None] * weights[:, None, :]).reshape(32, NIB * IBR)
    core_list = core.astype(jnp.int32).reshape(1)
    plane = ("y", "z")
    z_pair = lax.psum_scatter(z, "x", scatter_dimension=0, tiled=True)
    part = lax.all_to_all(part.reshape(16, 32, 640), plane, 0, 0, tiled=True).sum(0)
    part = jnp.broadcast_to(part[None], (4, 32, 640))
    part = lax.all_to_all(part, "x", 0, 0, tiled=True).sum(0)

    z_mine = jnp.where(first, z_pair[:128], z_pair[128:])
    z_theirs = swap_core(jnp.where(first, z_pair[128:], z_pair[:128]))
    z_left = jnp.where(first, z_mine, z_theirs)
    z_right = jnp.where(first, z_theirs, z_mine)
    y_first = -jnp.concatenate([z_left[:, :256], z_right[:, :256]], axis=1)
    z_second = jnp.concatenate([z_left[:, 256:], z_right[:, 256:]], axis=1)
    y_second = -(z_second + dot(y_first, link))
    shares = jnp.pad(dot(combine, y_second).reshape(16, 8, 128), ((0, 0), (0, 24), (0, 0)))
    message = jnp.concatenate([jnp.broadcast_to(part[None], (16, 32, 640)), shares], axis=2)
    message = lax.all_to_all(message, plane, 0, 0, tiled=True)
    gauge = message[:, :8, 640:].sum(0).reshape(2, 512)
    gauge = jnp.where(first, gauge[:1], gauge[1:]) + swap_core(
        jnp.where(first, gauge[1:], gauge[:1])
    )
    whole = message[:, :, :640].reshape(512, 640)
    diag_first, cross_second, diag_second = close(
        core_list, whole, swap_core(whole), diag_inverse, link
    )
    return (y_first, diag_first, y_second, cross_second, diag_second, gauge.reshape(1, 1, 512))


def solution(mesh):
    grid = Mesh(mesh.devices.reshape(4, 4, 4, 2), CHIPS + ("core",))
    in_specs = (
        P(COL, "x"),
        P(None, COL + ("x",), None),
        P(),
        P(),
        P(),
        P(COL, "x", None),
        P(COL, "x", None),
        P("x", COL, None),
    )
    out_specs = (
        P(COL + ("x",), None),
        P(),
        P(COL + ("x",), None),
        P(),
        P(),
        P("x", COL, None),
    )
    return jax.shard_map(local, mesh=grid, in_specs=in_specs, out_specs=out_specs, check_vma=False)
```

```python
import functools

import jax
import jax.numpy as jnp
from jax import lax
from jax.experimental import pallas as pl
from jax.experimental.pallas import tpu as pltpu
from jax.sharding import Mesh, PartitionSpec as P

NIB = 8
IBR = 16
HIGH = lax.Precision.HIGH
HIGHEST = lax.Precision.HIGHEST
COL = ("y", "z", "core")
CHIPS = ("x", "y", "z")
F32 = jnp.float32
BF16 = jnp.bfloat16


def dot(left, right, left_dim=1, right_dim=0, precision=HIGH):
    return lax.dot_general(
        left,
        right,
        (((left_dim,), (right_dim,)), ((), ())),
        precision=precision,
        preferred_element_type=F32,
    )


def swap_core(value):
    return lax.ppermute(value, "core", [(0, 1), (1, 0)])


def hop(value, leg, step):
    pairs = []
    for y in range(4):
        for z in range(4):
            for core in range(2):
                along_z = core == leg
                to_y, to_z = (y, (z + step) % 4) if along_z else ((y + step) % 4, z)
                pairs.append((y * 8 + z * 2 + core, to_y * 8 + to_z * 2 + core))
    return lax.ppermute(value, COL, pairs)


def parts(value):
    high = value.astype(BF16)
    return high, (value - high.astype(F32)).astype(BF16)


def product_kernel(count, has_total, has_gram, order, *refs):
    blocks, refs = refs[:4], refs[4:]
    pieces, refs = refs[:count], refs[count:]
    total, refs = (refs[0], refs[1:]) if has_total else (None, refs)
    rows, refs = (refs[0], refs[1:]) if has_gram else (None, refs)
    out, piece_high, piece_low = refs[0], refs[-2], refs[-1]
    step = pl.program_id(0)
    core = order[2 * pl.num_programs(0)]

    @pl.when(step == 0)
    def _():
        at = 0
        for piece in pieces:
            count_rows = piece.shape[0]
            to = slice(at, at + count_rows)
            piece_high[to, :], piece_low[to, :] = parts(piece[...])
            at += count_rows
        out[...] = total[...] if has_total else jnp.zeros_like(out)

    at = pl.ds(pl.multiple_of(step * 512, 512), 512)
    high, low = piece_high[at, :], piece_low[at, :]
    right = jnp.concatenate([high, low, high], axis=0)
    for one, two, side in ((blocks[0], blocks[1], core), (blocks[2], blocks[3], 1 - core)):
        one, two = parts(one[...]), parts(two[...])
        left = jnp.concatenate([one[0], two[0], one[0], two[0], one[1], two[1]], axis=1)
        made = jnp.dot(left, right, preferred_element_type=F32)
        for row in range(4):
            to = pl.ds(pl.multiple_of(row * 256 + side * 128, 128), 128)
            out[to, :] += made[row * 128 : row * 128 + 128, :]

    if has_gram:

        @pl.when(step == pl.num_programs(0) - 1)
        def _():
            gram_of(core == 0, rows, out, refs[1])


def add_product(order, mine, other, pieces, total=None, rows=None):
    depth = sum(piece.shape[0] for piece in pieces)
    one = pl.BlockSpec((512, 256), lambda j, order: (0, order[2 * j]))
    two = pl.BlockSpec((512, 256), lambda j, order: (0, order[2 * j + 1]))

    def fixed(shape):
        return pl.BlockSpec(shape, lambda j, order: (0, 0))

    made = fixed((1024, 512))
    has_total, has_gram = total is not None, rows is not None
    args = [order, mine, mine, other, other, *pieces]
    in_specs = [one, two, one, two] + [fixed(piece.shape) for piece in pieces]
    out_specs, out_shape = [made], [jax.ShapeDtypeStruct((1024, 512), F32)]
    if has_total:
        args.append(total)
        in_specs.append(made)
    if has_gram:
        args.append(rows)
        in_specs.append(fixed((1024, 1024)))
        out_specs.append(fixed((512, 640)))
        out_shape.append(jax.ShapeDtypeStruct((512, 640), F32))
    made = pl.pallas_call(
        functools.partial(product_kernel, len(pieces), has_total, has_gram),
        grid_spec=pltpu.PrefetchScalarGridSpec(
            num_scalar_prefetch=1,
            grid=(depth // 512,),
            in_specs=in_specs,
            out_specs=out_specs,
            scratch_shapes=[pltpu.VMEM((depth, 512), BF16)] * 2,
        ),
        out_shape=out_shape,
        cost_estimate=pl.CostEstimate(
            flops=6 * 1024 * 512 * depth, bytes_accessed=5120 * depth, transcendentals=0
        ),
        compiler_params=pltpu.CompilerParams(vmem_limit_bytes=48 << 20),
    )(*args)
    return made if has_gram else made[0]


def gram_of(first, rows, z, out):
    rows_high, rows_low = parts(rows[...])
    z_high, z_low = parts(z[...])

    def product(left, right):
        def terms(one, two):
            return lax.dot_general(one, two, (((0,), (0,)), ((), ())), preferred_element_type=F32)

        return terms(left[0], right[0]) + terms(left[0], right[1]) + terms(left[1], right[0])

    def panel(start, stop):
        return rows_high[:, start:stop], rows_low[:, start:stop]

    def kept(start, stop):
        return z_high[:, start:stop], z_low[:, start:stop]

    def either(one, two):
        return tuple(jnp.where(first, left, right) for left, right in zip(one, two))

    out[:, :256] = product(panel(0, 512), kept(256, 512))
    for slot in range(2):
        at, start, half = slice(slot * 256, slot * 256 + 256), slot * 512, slot * 256
        low, high = panel(start, start + 256), panel(start + 256, start + 512)
        mine = kept(half, half + 256)
        out[at, 256:512] = product(either(low, high), mine)
        out[at, 512:] = product(
            either(high, mine), either(kept(half, half + 128), panel(start + 128, start + 256))
        )


def close_kernel(core, mine, theirs, diag, link, diag_first, cross_second, diag_second):
    first = core[0] == 0

    def sides(rows, columns):
        kept, came = mine[rows, columns], theirs[rows, columns]
        return jnp.where(first, kept, came), jnp.where(first, came, kept)

    def symmetric(slot):
        rows = slice(slot * 256, slot * 256 + 256)
        upper, lower = sides(rows, slice(256, 512))
        below = jnp.concatenate(sides(rows, slice(512, 640)), axis=1)
        return jnp.concatenate(
            [
                jnp.concatenate([upper, below.T], axis=1),
                jnp.concatenate([below, lower], axis=1),
            ],
            axis=0,
        )

    def product(left, right, dim=1):
        def terms(one, two):
            return lax.dot_general(one, two, (((dim,), (0,)), ((), ())), preferred_element_type=F32)

        left, right = parts(left), parts(right)
        return terms(left[0], right[0]) + terms(left[0], right[1]) + terms(left[1], right[0])

    cross = jnp.concatenate(sides(slice(0, 512), slice(0, 256)), axis=1)
    links = link[...]
    top = diag[0] + symmetric(0)
    diag_first[...] = top
    second = cross - product(top, links)
    cross_second[...] = second
    diag_second[...] = (
        diag[1] + symmetric(1) - product(cross, links, 0) - product(links, second, 0)
    )


def close(core, mine, theirs, diag, link):
    return pl.pallas_call(
        close_kernel,
        in_specs=[pl.BlockSpec(memory_space=pltpu.SMEM)]
        + [pl.BlockSpec(memory_space=pltpu.VMEM)] * 4,
        out_shape=[jax.ShapeDtypeStruct((512, 512), F32)] * 3,
        cost_estimate=pl.CostEstimate(
            flops=36 * 512 * 512 * 512, bytes_accessed=9 << 20, transcendentals=0
        ),
        compiler_params=pltpu.CompilerParams(vmem_limit_bytes=40 << 20),
    )(core, mine, theirs, diag, link)


def local(
    ancestor,
    panels,
    pattern,
    diag_inverse,
    link,
    block_list,
    gauge_owner,
    gauge_weight,
):
    row = lax.axis_index("x")
    place_y, place_z, core = (lax.axis_index(name) for name in COL)
    first = core == 0
    col = place_y * 8 + place_z * 2 + core
    flags = lax.dynamic_index_in_dim(pattern, col * 4 + row, 1, keepdims=False).astype(F32)
    tiles = panels.reshape(2, 128, 2, 256) * flags[:, None, :, None]
    left, right = tiles[:, :, 0], tiles[:, :, 1]
    theirs = swap_core(jnp.where(first, right, left))
    mine = jnp.where(first, left, right)
    own = jnp.concatenate([jnp.where(first, mine, theirs), jnp.where(first, theirs, mine)], axis=1)
    ancestor, theirs = lax.optimization_barrier((ancestor, theirs))
    other = swap_core(ancestor)

    def order_of(*offsets):
        order = []
        for leg_0, leg_1 in offsets:
            step_y = jnp.where(first, leg_1, leg_0)
            step_z = jnp.where(first, leg_0, leg_1)
            order.append(((place_y + step_y) % 4) * 4 + (place_z + step_z) % 4)
        return jnp.stack(order + [core]).astype(jnp.int32)

    both = jnp.concatenate([left[0], right[0], left[1], right[1]], axis=1)
    rows = lax.all_gather(both, ("x", "core"), axis=0, tiled=True)
    own = jnp.concatenate([own[0], own[1]], axis=1)
    behind = hop(own, 0, 1)
    ahead = hop(own, 0, -1)
    across = hop(own, 0, 2)
    pair = jnp.concatenate([own, behind], axis=0)
    pair_behind = hop(pair, 1, 1)
    pair_ahead = hop(pair, 1, -1)
    rest = jnp.concatenate([ahead, across], axis=0)
    rest_behind = hop(rest, 1, 1)
    rest_ahead = hop(rest, 1, -1)
    z = add_product(order_of((0, 0), (-1, 0), (1, 0), (2, 0)), ancestor, other, (pair, rest))
    pair_behind, z = lax.optimization_barrier((pair_behind, z))
    pair_across = hop(pair_behind, 1, 1)
    z = add_product(
        order_of((0, -1), (-1, -1), (0, 1), (-1, 1)), ancestor, other, (pair_behind, pair_ahead), z
    )
    weights = gauge_weight.reshape(32, IBR)
    rest_ahead, z, weights = lax.optimization_barrier((rest_ahead, z, weights))
    rest_across = hop(rest_ahead, 1, -1)
    weights = lax.all_to_all(weights, COL, 0, 0, tiled=True)
    z = add_product(
        order_of((1, -1), (2, -1), (1, 1), (2, 1), (0, 2), (-1, 2)),
        ancestor,
        other,
        (rest_behind, rest_ahead, pair_across),
        z,
    )
    z, rows, weights = lax.optimization_barrier((z, rows, weights))
    z, part = add_product(
        order_of((1, 2), (2, 2)), ancestor, other, (rest_across,), z, rows
    )

    owner_match = (
        gauge_owner[0, 0][None, :] == jnp.arange(32, dtype=jnp.int32)[:, None]
    ).astype(F32)
    block_match = (
        block_list[0, 0][:, None] == jnp.arange(NIB, dtype=jnp.int32)[None, :]
    ).astype(F32)
    selector = dot(owner_match, block_match, precision=HIGHEST)
    combine = (selector[:, :, None] * weights[:, None, :]).reshape(32, NIB * IBR)
    core_list = core.astype(jnp.int32).reshape(1)
    plane = ("y", "z")
    z_pair = lax.psum_scatter(z, "x", scatter_dimension=0, tiled=True)
    part = lax.all_to_all(part.reshape(16, 32, 640), plane, 0, 0, tiled=True).sum(0)
    part = jnp.broadcast_to(part[None], (4, 32, 640))
    part = lax.all_to_all(part, "x", 0, 0, tiled=True).sum(0)

    z_mine = jnp.where(first, z_pair[:128], z_pair[128:])
    z_theirs = swap_core(jnp.where(first, z_pair[128:], z_pair[:128]))
    z_left = jnp.where(first, z_mine, z_theirs)
    z_right = jnp.where(first, z_theirs, z_mine)
    y_first = -jnp.concatenate([z_left[:, :256], z_right[:, :256]], axis=1)
    z_second = jnp.concatenate([z_left[:, 256:], z_right[:, 256:]], axis=1)
    y_second = -(z_second + dot(y_first, link))
    shares = jnp.pad(dot(combine, y_second).reshape(16, 8, 128), ((0, 0), (0, 24), (0, 0)))
    message = jnp.concatenate([jnp.broadcast_to(part[None], (16, 32, 640)), shares], axis=2)
    message = lax.all_to_all(message, plane, 0, 0, tiled=True)
    gauge = message[:, :8, 640:].sum(0).reshape(2, 512)
    gauge = jnp.where(first, gauge[:1], gauge[1:]) + swap_core(
        jnp.where(first, gauge[1:], gauge[:1])
    )
    whole = message[:, :, :640].reshape(512, 640)
    diag_first, cross_second, diag_second = close(
        core_list, whole, swap_core(whole), diag_inverse, link
    )
    return (y_first, diag_first, y_second, cross_second, diag_second, gauge.reshape(1, 1, 512))


def solution(mesh):
    grid = Mesh(mesh.devices.reshape(4, 4, 4, 2), CHIPS + ("core",))
    in_specs = (
        P(COL, "x"),
        P(None, COL + ("x",), None),
        P(),
        P(),
        P(),
        P(COL, "x", None),
        P(COL, "x", None),
        P("x", COL, None),
    )
    out_specs = (
        P(COL + ("x",), None),
        P(),
        P(COL + ("x",), None),
        P(),
        P(),
        P("x", COL, None),
    )
    return jax.shard_map(local, mesh=grid, in_specs=in_specs, out_specs=out_specs, check_vma=False)
```
